256 devices in a mesh: grp: 4 (over x), own: 64 (over z, y, core).
Axes of the slice: x: 4, y: 4, z: 8, core: 2. Of those that a mesh axis runs over, the one named last changes fastest.
Arguments:
- coefficients: bfloat16 [64, 1024, 4608], P('own', 'grp'), parts along dimension 1, may hold values from -6 to 6
- rotations: bfloat16 [64, 3342336], P('own'), may hold values from -0.75 to 0.75
- legendre: bfloat16 [256, 512, 512], P('own'), may hold values from -48 to 48, as said below
- degree_slot: int32 [8, 64], replicated, may hold values from 0 to 63, each once within a row
- column_order: int32 [1024], P('grp'), parts along dimension 0, may hold values from 0 to 255, each once
Outputs:
- grid_errors: bfloat16 [1024, 256, 1024], P('grp', 'own'), parts along dimension 0
The draws below stay inside these ranges and needn't reach their ends.
There are 4 independent parts, one for each index of `grp`. The reference program is written for one: setup_inputs(seed, part) draws one part's arguments, and reference() takes and returns one part's arrays. A program takes and returns all parts, laid end to end along the dimension named above; an argument that names none is the same for every part. Nothing has to cross between parts.
Inputs may be any that keep to these rules, and one draw needn't show every extreme that they name: Each row is a permutation; slot s of class k holds degree 64 * k + degree_slot[k, s]. `column_order`: a permutation of the columns. legendre[t, m, l] is zero where l < m.
All inputs are finite; a program needn't handle non-finite values.
Results may differ from the reference program's by a relative error of at most 0.0062.
Values may be sent and summed in bfloat16 or wider, within the bound.
No kernel may reach another device: no remote copies, remote signals or barrier semaphores. Data moves between devices by JAX's collectives and lax.ppermute only.
A program may use at most 128 MiB of HBM per device.

```python
import math
import jax
import jax.numpy as jnp
from jax import lax

SLOTS = 64
CLASSES = 8
NLAT = 256
ORDERS = 512
NLON = 1024
COLUMNS = 256
SLOT_ROWS = 4608
ROT_SLOT = 3342336


def draw_rotations(key, part):
    flat = jnp.arange(ROT_SLOT, dtype=jnp.int32)
    bucket = jnp.zeros((ROT_SLOT,), jnp.int32)
    for upper in range(1, CLASSES):
        limit = 4 * SLOTS * SLOTS * upper * (upper + 1) * (2 * upper + 1) // 6
        bucket = bucket + (flat >= limit).astype(jnp.int32)
    spread = 1.0 / jnp.sqrt((2 * SLOTS * (bucket + 1) - SLOTS).astype(jnp.float32))
    values = jax.random.truncated_normal(key, -6.0, 6.0, (SLOTS, ROT_SLOT), jnp.float32)
    return (values * spread[None, :]).astype(jnp.bfloat16)


def legendre_table(colatitude):
    orders = SLOTS * CLASSES
    order_float = jnp.arange(orders, dtype=jnp.float32)
    sines = jnp.sin(colatitude)
    cosines = jnp.cos(colatitude)
    growth = 0.5 * jnp.log((2.0 * order_float + 1.0) / jnp.maximum(2.0 * order_float, 1.0))
    doubling = jnp.where(order_float >= 1.0, 0.5 * math.log(2.0), 0.0)
    log_seed = (jnp.cumsum(growth) + doubling)[:, None] + order_float[:, None] * jnp.log(sines)[None, :]
    seeds = jnp.exp(log_seed)
    squared = order_float * order_float

    def advance(carry, degree):
        previous, earlier = carry
        degree_float = degree.astype(jnp.float32)
        above = degree_float > order_float
        deeper = degree_float > order_float + 1.0
        leading = jnp.sqrt(jnp.where(above, (4.0 * degree_float * degree_float - 1.0) / jnp.where(above, degree_float * degree_float - squared, 1.0), 0.0))
        lowered = degree_float - 1.0
        trailing = jnp.sqrt(jnp.where(deeper, (lowered * lowered - squared) / jnp.where(deeper, 4.0 * lowered * lowered - 1.0, 1.0), 0.0))
        recursed = leading[:, None] * (cosines[None, :] * previous - trailing[:, None] * earlier)
        current = jnp.where(above[:, None], recursed, jnp.where((degree_float == order_float)[:, None], seeds, 0.0))
        return ((current, previous), current)
    initial = jnp.zeros((orders, colatitude.shape[0]), jnp.float32)
    final, values = lax.scan(advance, (initial, initial), jnp.arange(orders, dtype=jnp.int32))
    return jnp.transpose(values, (2, 1, 0))


def draw_legendre(key, part):
    colatitude = jax.random.uniform(key, (NLAT,), jnp.float32, 0.15, math.pi - 0.15)
    return legendre_table(colatitude).astype(jnp.bfloat16)


def steps_of(key, shape, cuts, smallest, largest):
    gain = 1.0
    for dim, blocks in cuts:
        heights = jax.random.uniform(jax.random.fold_in(jax.random.fold_in(key, 6), dim), (blocks,), jnp.float32, smallest / len(cuts), largest / len(cuts))
        gain = gain * jnp.repeat(jnp.exp(heights), shape[dim] // blocks).reshape((-1,) + (1,) * (len(shape) - 1 - dim))
    return gain


def normal_values(own_key, dims, width, most, split=(), held_as=jnp.bfloat16):
    loudness = steps_of(own_key, dims, split, -0.22, 0.18) if split else 1.0
    drawn = jax.random.normal(own_key, dims, jnp.float32) * width * loudness
    return jnp.minimum(jnp.maximum(drawn, -most), most).astype(held_as)


def setup_inputs(seed: int = 0, part: int = 0) -> dict:
    arg_keys = jax.random.split(jax.random.key(seed), 6)
    own_keys = jax.random.split(jax.random.fold_in(arg_keys[5], part), 6)
    coefficients = normal_values(own_keys[0], (SLOTS, COLUMNS, SLOT_ROWS), 1.0, 6.0, ((0, 64),))
    rotations = draw_rotations(jax.random.fold_in(arg_keys[5], 71), part)
    legendre = draw_legendre(jax.random.fold_in(arg_keys[5], 71), part)
    degree_slot = jax.vmap(lambda own: jax.random.permutation(own, SLOTS))(jax.random.split(arg_keys[3], CLASSES)).reshape((CLASSES, SLOTS)).astype(jnp.int32)
    column_order = jax.random.permutation(own_keys[4], COLUMNS).astype(jnp.int32)
    return {"coefficients": coefficients, "rotations": rotations, "legendre": legendre, "degree_slot": degree_slot, "column_order": column_order}


def rotate_bucket(selected, rotations, degrees, bucket):
    extent = 2 * SLOTS * (bucket + 1)
    first_row = SLOTS * bucket * (bucket + 1)
    offset = 4 * SLOTS * SLOTS * bucket * (bucket + 1) * (2 * bucket + 1) // 6
    block = selected[:, :, first_row:first_row + extent].astype(jnp.float32)
    active = jnp.arange(extent, dtype=jnp.int32)[None, :] < (2 * degrees + 1)[:, None]
    block = jnp.where(active[:, None, :], block, jnp.zeros((), jnp.float32))
    matrix = rotations[:, offset:offset + extent * extent].reshape(SLOTS, extent, extent).astype(jnp.float32)
    turned = jnp.einsum("sij,scj->sic", matrix, block)
    return turned.astype(jnp.bfloat16)


def order_entries(turned, degrees, order_ids):
    extent = turned.shape[1]
    upward = degrees[:, None] + order_ids[None, :]
    downward = degrees[:, None] - order_ids[None, :]
    upward_valid = order_ids[None, :] <= degrees[:, None]
    downward_valid = upward_valid & (order_ids[None, :] >= 1)
    cosine = jnp.take_along_axis(turned, jnp.clip(upward, 0, extent - 1)[:, :, None], axis=1)
    sine_part = jnp.take_along_axis(turned, jnp.clip(downward, 0, extent - 1)[:, :, None], axis=1)
    nothing = jnp.zeros((), turned.dtype)
    cosine = jnp.where(upward_valid[:, :, None], cosine, nothing)
    sine_part = jnp.where(downward_valid[:, :, None], sine_part, nothing)
    return jnp.stack([cosine, sine_part], axis=2)


def synthesize_order(inputs):
    legendre_rows, coefficient_rows = inputs
    return jnp.dot(legendre_rows, coefficient_rows, preferred_element_type=jnp.float32).astype(jnp.bfloat16)


def reference(coefficients, rotations, legendre, degree_slot, column_order):
    selected = jnp.take(coefficients, column_order, axis=1)
    order_ids = jnp.arange(ORDERS, dtype=jnp.int32)
    pieces = []
    degree_lists = []
    for bucket in range(CLASSES):
        degrees = (SLOTS * bucket + degree_slot[bucket]).astype(jnp.int32)
        degree_lists.append(degrees)
        turned = rotate_bucket(selected, rotations, degrees, bucket)
        pieces.append(order_entries(turned, degrees, order_ids))
    stacked = jnp.concatenate(pieces, axis=0)
    by_order = jnp.transpose(stacked, (1, 0, 2, 3)).reshape(ORDERS, CLASSES * SLOTS, 2 * COLUMNS)
    degree_index = jnp.concatenate(degree_lists).astype(jnp.int32)
    legendre_slots = jnp.take(legendre, degree_index, axis=2)
    legendre_orders = jnp.transpose(legendre_slots, (1, 0, 2))
    fourier = lax.map(synthesize_order, (legendre_orders, by_order))
    fourier = fourier.reshape(ORDERS, NLAT, 2, COLUMNS)
    fourier = jnp.transpose(fourier, (1, 0, 2, 3)).reshape(NLAT, 2 * ORDERS, COLUMNS)
    longitude = jnp.arange(NLON, dtype=jnp.int32)
    product_mod = (order_ids[:, None] * longitude[None, :]) % NLON
    angles = product_mod.astype(jnp.float32) * (2.0 * math.pi / NLON)
    wave = (jnp.stack([jnp.cos(angles), jnp.sin(angles)], axis=1) / ORDERS).astype(jnp.bfloat16)
    wave = wave.reshape(2 * ORDERS, NLON)

    def transform_latitude(rows):
        return jnp.dot(rows.T, wave, preferred_element_type=jnp.float32).astype(jnp.bfloat16)

    grid = lax.map(transform_latitude, fourier)
    return jnp.transpose(grid, (1, 0, 2))
```

```python
import functools
import math

import jax
import jax.numpy as jnp
from jax import lax
from jax.experimental import pallas as pl
from jax.experimental.pallas import tpu as pltpu
from jax.sharding import PartitionSpec as P

SLOTS = 64
CLASSES = 8
COLUMNS = 256
ORDERS = SLOTS * CLASSES
NLON = 2 * ORDERS
PAIRED = CLASSES // 2
WIDE = 2 * COLUMNS
PACKED = PAIRED * WIDE + COLUMNS
FRONT = SLOTS * CLASSES
BF = jnp.bfloat16
F32 = jnp.float32
VMEM_LIMIT = 60 * 1024 * 1024


def extent(k):
    return 2 * SLOTS * (k + 1)


def first_row(k):
    return SLOTS * k * (k + 1)


def rotation_offset(k):
    return 4 * SLOTS * SLOTS * k * (k + 1) * (2 * k + 1) // 6


def packed_rows(group):
    if group == 0:
        return [(r, 0) for r in range(CLASSES)]
    other = CLASSES - group
    return [(r, group) if r >= group else (r + other, other) for r in range(CLASSES)]


def interleave(reverse_from):
    size = CLASSES * SLOTS
    row = lax.broadcasted_iota(jnp.int32, (size, size), 0)
    col = lax.broadcasted_iota(jnp.int32, (size, size), 1)
    d = row // CLASSES
    r = row % CLASSES
    d = jnp.where(r >= reverse_from, SLOTS - 1 - d, d)
    return jnp.where(col == r * SLOTS + d, 1.0, 0.0).astype(BF)


def rotate_kernel(deg_ref, order_ref, coef_ref, rot_ref, out_ref, *scratch):
    flats = scratch[:CLASSES]
    wide = scratch[CLASSES : CLASSES + 2]
    turned = scratch[CLASSES + 2 : CLASSES + 4]
    y_ref, sems = scratch[CLASSES + 4 :]
    own = lax.axis_index("own")
    copies = []
    for k in range(CLASSES):
        size = extent(k) * extent(k)
        copy = pltpu.make_async_copy(
            rot_ref.at[:, pl.ds(rotation_offset(k), size)], flats[k], sems.at[k]
        )
        copy.start()
        copies.append(copy)
    chosen = lax.broadcasted_iota(jnp.int32, (COLUMNS, COLUMNS), 0) == order_ref[...]
    chosen = jnp.where(chosen, 1.0, 0.0).astype(BF)
    for k in range(CLASSES):
        n = extent(k)
        rows = n * (k + 1)
        v_ref = wide[k % 2]
        r_ref = turned[k % 2]
        copies[k].wait()
        v_ref[FRONT : FRONT + rows, :] = flats[k][...].astype(F32).reshape(rows, 128)
        slot_degree = deg_ref[k, own]
        degree = SLOTS * k + slot_degree
        for j in range(k + 1):
            for p in range(2):
                start = degree + SLOTS * j if p == 0 else degree - SLOTS * j - (SLOTS - 1)
                base = FRONT + start * (k + 1)
                at = (2 * j + p) * SLOTS
                for a in range(k + 1):
                    if k == 0:
                        window = v_ref[pl.ds(base, SLOTS), :]
                    else:
                        window = v_ref[pl.ds(base + a, SLOTS, stride=k + 1), :]
                    r_ref[at : at + SLOTS, a * 128 : (a + 1) * 128] = window.astype(BF)
        block = coef_ref[:, first_row(k) : first_row(k) + n]
        lane = lax.broadcasted_iota(jnp.int32, (COLUMNS, n), 1)
        block = jnp.where(lane < 2 * degree + 1, block, jnp.zeros((), BF))
        y = lax.dot_general(
            r_ref[:n, :n], block, (((1,), (1,)), ((), ())), preferred_element_type=F32
        ).astype(BF)
        row = lax.broadcasted_iota(jnp.int32, (SLOTS, COLUMNS), 0)
        y = jnp.dot(y, chosen, preferred_element_type=F32)
        base = first_row(k)
        for j in range(k + 1):
            for p in range(2):
                at = (2 * j + p) * SLOTS
                part = y[at : at + SLOTS, :]
                order = row if p == 0 else SLOTS - 1 - row
                if j == k:
                    part = jnp.where(order <= slot_degree, part, 0.0)
                if j == 0 and p == 1:
                    part = jnp.where(order >= 1, part, 0.0)
                y_ref[base + at : base + at + SLOTS, :] = part.astype(BF)

    def piece(k, j, p):
        at = first_row(k) + (2 * j + p) * SLOTS
        return y_ref[at : at + SLOTS, :]

    for p in range(2):
        perm = interleave(CLASSES if p == 0 else 0)
        for group in range(PAIRED):
            stacked = jnp.concatenate([piece(k, j, p) for k, j in packed_rows(group)], axis=0)
            lanes = group * WIDE + p * COLUMNS
            out_ref[:, lanes : lanes + COLUMNS] = jnp.dot(
                perm, stacked, preferred_element_type=F32
            ).astype(BF)
    stacked = jnp.concatenate(
        [piece(k, PAIRED, p) for p in range(2) for k in range(PAIRED, CLASSES)], axis=0
    )
    out_ref[:, PAIRED * WIDE :] = jnp.dot(
        interleave(PAIRED), stacked, preferred_element_type=F32
    ).astype(BF)


def rotate(degree_slot, column_order, coefficients, rotations):
    scratch = [pltpu.VMEM((1, extent(k) * extent(k)), BF) for k in range(CLASSES)]
    top = extent(CLASSES - 1)
    scratch += [pltpu.VMEM((FRONT + top * CLASSES, 128), F32)] * 2
    scratch += [pltpu.VMEM((top, top), BF)] * 2
    scratch += [
        pltpu.VMEM((first_row(CLASSES), COLUMNS), BF),
        pltpu.SemaphoreType.DMA((CLASSES,)),
    ]
    return pl.pallas_call(
        rotate_kernel,
        out_shape=jax.ShapeDtypeStruct((CLASSES * SLOTS, PACKED), BF),
        in_specs=[
            pl.BlockSpec(memory_space=pltpu.SMEM),
            pl.BlockSpec(memory_space=pltpu.VMEM),
            pl.BlockSpec(memory_space=pltpu.VMEM),
            pl.BlockSpec(memory_space=pl.ANY),
        ],
        out_specs=pl.BlockSpec(memory_space=pltpu.VMEM),
        scratch_shapes=scratch,
        compiler_params=pltpu.CompilerParams(vmem_limit_bytes=VMEM_LIMIT),
        cost_estimate=pl.CostEstimate(
            flops=4 * 10**9, bytes_accessed=18 * 10**6, transcendentals=0
        ),
        name="rotate",
    )(degree_slot, column_order, coefficients, rotations)


def legendre_kernel(grp_ref, targets_ref, *refs):
    pieces = refs[:4]
    out_ref, rows_ref = refs[4:]
    for back in range(4):
        group = lax.rem(grp_ref[0] + 4 - back, 4)
        rows_ref[pl.ds(pl.multiple_of(group * SLOTS, SLOTS), SLOTS), :] = pieces[back][...]
    size = CLASSES * SLOTS

    def one_hot(which, depth):
        row = lax.broadcasted_iota(jnp.int32, (depth, size), 0)
        return jnp.where(row == targets_ref[which : which + 1, :], 1.0, 0.0).astype(BF)

    def put(at, left, right):
        out_ref[at * 4 * SLOTS : (at + 1) * 4 * SLOTS, :] = jnp.dot(
            left, right, preferred_element_type=F32
        ).astype(BF)

    main = one_hot(0, size)
    lane = lax.broadcasted_iota(jnp.int32, (4 * SLOTS, size), 1)
    for j in range(PAIRED):
        values = rows_ref[:, j * size : (j + 1) * size]
        kept = values
        if j:
            kept = jnp.where(lane >= SLOTS * j, values, jnp.zeros((), BF))
            put(PAIRED + 1 + CLASSES - j - PAIRED, values, one_hot(j, size))
        put(j, kept, main)
    values = rows_ref[:, PAIRED * size :]
    for p in range(2):
        put(PAIRED + p, values, one_hot(PAIRED + p, size // 2))


def legendre_rows(grp, targets, pieces):
    size = CLASSES * SLOTS
    return pl.pallas_call(
        legendre_kernel,
        out_shape=jax.ShapeDtypeStruct(((CLASSES + 1) * 4 * SLOTS, size), BF),
        in_specs=[pl.BlockSpec(memory_space=pltpu.SMEM)]
        + [pl.BlockSpec(memory_space=pltpu.VMEM)] * 5,
        out_specs=pl.BlockSpec(memory_space=pltpu.VMEM),
        scratch_shapes=[pltpu.VMEM((4 * SLOTS, PAIRED * size + size // 2), BF)],
        compiler_params=pltpu.CompilerParams(vmem_limit_bytes=VMEM_LIMIT),
        cost_estimate=pl.CostEstimate(flops=10**9, bytes_accessed=4 * 10**6, transcendentals=0),
        name="legendre",
    )(grp, targets, *pieces)


def synthesize_kernel(x_ref, l_ref, out_ref, f_ref):
    size = CLASSES * SLOTS
    tall = 4 * SLOTS

    def put(j, left, lanes, width, at):
        summed = jnp.dot(
            l_ref[left * tall : (left + 1) * tall, :],
            x_ref[:, lanes : lanes + width],
            preferred_element_type=F32,
        ).astype(BF)
        for g in range(4):
            f_ref[g, j * SLOTS : (j + 1) * SLOTS, at : at + width] = summed[
                g * SLOTS : (g + 1) * SLOTS, :
            ]

    for j in range(CLASSES):
        if j < PAIRED:
            put(j, j, j * WIDE, WIDE, 0)
        elif j == PAIRED:
            for p in range(2):
                put(j, PAIRED + p, PAIRED * WIDE, COLUMNS, p * COLUMNS)
        else:
            put(j, j + 1, (CLASSES - j) * WIDE, WIDE, 0)
    perm = interleave(CLASSES)
    for g in range(4):
        out_ref[:, g * WIDE : (g + 1) * WIDE] = jnp.dot(
            perm, f_ref[g], preferred_element_type=F32
        ).astype(BF)


def synthesize(packed, rows):
    size = CLASSES * SLOTS
    return pl.pallas_call(
        synthesize_kernel,
        out_shape=jax.ShapeDtypeStruct((size, 4 * WIDE), BF),
        in_specs=[pl.BlockSpec(memory_space=pltpu.VMEM)] * 2,
        out_specs=pl.BlockSpec(memory_space=pltpu.VMEM),
        scratch_shapes=[pltpu.VMEM((4, size, WIDE), BF)],
        compiler_params=pltpu.CompilerParams(vmem_limit_bytes=VMEM_LIMIT),
        cost_estimate=pl.CostEstimate(
            flops=2 * 10**9, bytes_accessed=7 * 10**6, transcendentals=0
        ),
        name="synthesize",
    )(packed, rows)


def transform_kernel(x_ref, w_ref, out_ref, y_ref):
    for g in range(4):
        total = None
        for p in range(2):
            lanes = g * WIDE + p * COLUMNS
            part = lax.dot_general(
                x_ref[:, lanes : lanes + COLUMNS],
                w_ref[p],
                (((0,), (0,)), ((), ())),
                preferred_element_type=F32,
            )
            total = part if total is None else total + part
        for i in range(NLON // 128):
            y_ref[i, pl.ds(g, COLUMNS, stride=4), :] = total[:, i * 128 : (i + 1) * 128]
    for i in range(NLON // 128):
        out_ref[:, :, i * 128 : (i + 1) * 128] = (
            y_ref[i].reshape(COLUMNS, 4, 128).astype(BF)
        )


def transform(received, wave):
    return pl.pallas_call(
        transform_kernel,
        out_shape=jax.ShapeDtypeStruct((COLUMNS, 4, NLON), BF),
        in_specs=[pl.BlockSpec(memory_space=pltpu.VMEM)] * 2,
        out_specs=pl.BlockSpec(memory_space=pltpu.VMEM),
        scratch_shapes=[pltpu.VMEM((NLON // 128, 4 * COLUMNS, 128), F32)],
        compiler_params=pltpu.CompilerParams(vmem_limit_bytes=VMEM_LIMIT),
        cost_estimate=pl.CostEstimate(
            flops=2 * 10**9, bytes_accessed=7 * 10**6, transcendentals=0
        ),
        name="transform",
    )(received, wave)


def wave_table():
    row = jnp.arange(ORDERS, dtype=jnp.int32)
    order = SLOTS * (row % CLASSES) + row // CLASSES
    longitude = jnp.arange(NLON, dtype=jnp.int32)
    angles = (order[:, None] * longitude[None, :] % NLON).astype(F32) * (2.0 * math.pi / NLON)
    return (jnp.stack([jnp.cos(angles), jnp.sin(angles)], axis=0) / ORDERS).astype(BF)


def one_hot_targets(degree_slot):
    slot_major = degree_slot.T
    row = jnp.arange(CLASSES, dtype=jnp.int32)[None, :]
    main = slot_major + SLOTS * row
    targets = [main]
    for group in range(1, PAIRED):
        other = CLASSES - group
        shifted = jnp.roll(slot_major, -other, axis=1) + SLOTS * row
        targets.append(jnp.where(row < group, shifted, -1))
    half = jnp.roll(slot_major, -PAIRED, axis=1) + SLOTS * row
    targets.append(jnp.where(row < PAIRED, half, -1))
    half = slot_major + SLOTS * (row - PAIRED)
    targets.append(jnp.where(row >= PAIRED, half, -1))
    targets += [main, main]
    return jnp.stack(targets, axis=0).reshape(CLASSES, CLASSES * SLOTS)


def pack_legendre(latitude):
    by_class = latitude.reshape(CLASSES, SLOTS, ORDERS)
    groups = [by_class[0]]
    lane = jnp.arange(ORDERS, dtype=jnp.int32)[None, :]
    for group in range(1, PAIRED):
        other = jnp.roll(by_class[CLASSES - group], SLOTS * group, axis=1)
        groups.append(jnp.where(lane < SLOTS * group, other, by_class[group]))
    groups.append(by_class[PAIRED][:, SLOTS * PAIRED :])
    return jnp.concatenate(groups, axis=1)


def local(coefficients, rotations, legendre, degree_slot, column_order):
    grp = lax.axis_index("grp")
    latitude = lax.dynamic_index_in_dim(legendre, grp, axis=0, keepdims=False)
    sent = pack_legendre(latitude).reshape(SLOTS, 2, -1)
    mine = lax.all_to_all(sent, "own", split_axis=0, concat_axis=0, tiled=True)
    pieces = [mine]
    for shift in range(1, 4):
        pieces.append(lax.ppermute(mine, "grp", [(i, (i + shift) % 4) for i in range(4)]))
    pieces = [piece.reshape(SLOTS, -1) for piece in pieces]
    rows = legendre_rows(grp.reshape(1), one_hot_targets(degree_slot), pieces)

    outgoing = rotate(
        degree_slot,
        column_order.reshape(1, -1),
        coefficients.reshape(COLUMNS, -1),
        rotations,
    )
    packed = lax.all_to_all(
        outgoing.reshape(SLOTS, CLASSES, PACKED), "own", split_axis=0, concat_axis=0, tiled=True
    )
    fourier = synthesize(packed.reshape(SLOTS * CLASSES, PACKED), rows)
    received = lax.all_to_all(
        fourier.reshape(SLOTS, CLASSES, 4 * WIDE), "own", split_axis=0, concat_axis=0, tiled=True
    )
    return transform(received.reshape(SLOTS * CLASSES, 4 * WIDE), wave_table())


def solution(mesh):
    placed = (P("own", "grp", None), P("own", None), P("own", None, None), P(), P("grp"))
    return jax.shard_map(
        local, mesh=mesh, in_specs=placed, out_specs=P("grp", "own", None), check_vma=False
    )
```

```python
import functools
import math

import jax
import jax.numpy as jnp
from jax import lax
from jax.experimental import pallas as pl
from jax.experimental.pallas import tpu as pltpu
from jax.sharding import PartitionSpec as P

SLOTS = 64
CLASSES = 8
COLUMNS = 256
ORDERS = SLOTS * CLASSES
NLON = 2 * ORDERS
PAIRED = CLASSES // 2
WIDE = 2 * COLUMNS
STEPS = 2
GROUP = 2
OUTS = 2
PACKED = PAIRED * WIDE + COLUMNS
FRONT = SLOTS * CLASSES
BLOCKS = (PAIRED * ORDERS + ORDERS // 2) // 128
BF = jnp.bfloat16
F32 = jnp.float32
MIB = 1024 * 1024


def extent(k):
    return 2 * SLOTS * (k + 1)


def first_row(k):
    return SLOTS * k * (k + 1)


def rotation_offset(k):
    return 4 * SLOTS * SLOTS * k * (k + 1) * (2 * k + 1) // 6


def packed_rows(group):
    if group == 0:
        return [(r, 0) for r in range(CLASSES)]
    other = CLASSES - group
    return [(r, group) if r >= group else (r + other, other) for r in range(CLASSES)]


def interleave(reverse_from):
    size = CLASSES * SLOTS
    row = lax.broadcasted_iota(jnp.int32, (size, size), 0)
    col = lax.broadcasted_iota(jnp.int32, (size, size), 1)
    d = row // CLASSES
    r = row % CLASSES
    d = jnp.where(r >= reverse_from, SLOTS - 1 - d, d)
    return jnp.where(col == r * SLOTS + d, 1.0, 0.0).astype(BF)


def rotate_kernel(deg_ref, coef_hbm, rot_ref, out_hbm, *scratch):
    flats = scratch[:CLASSES]
    wide = scratch[CLASSES : CLASSES + 2]
    coef_ref, y_ref, out_ref, sems = scratch[CLASSES + 2 :]
    own = lax.axis_index("own")
    copies = []
    first = pltpu.make_async_copy(coef_hbm, coef_ref, sems.at[CLASSES])
    for k in range(CLASSES):
        size = extent(k) * extent(k)
        copies.append(
            pltpu.make_async_copy(
                rot_ref.at[:, pl.ds(rotation_offset(k), size)], flats[k], sems.at[k]
            )
        )
    for at, k in enumerate(range(CLASSES)):
        copies[k].start()
        if at == 1:
            first.start()
    row = lax.broadcasted_iota(jnp.int32, (SLOTS, COLUMNS), 0)
    for at, k in enumerate(range(CLASSES)):
        n = extent(k)
        rows = n * (k + 1)
        v_ref = wide[at % 2]
        copies[k].wait()
        v_ref[FRONT : FRONT + rows, :] = flats[k][...].astype(F32).reshape(rows, 128)
        slot_degree = deg_ref[k, own]
        degree = SLOTS * k + slot_degree
        if k == 0:
            first.wait()
        block = coef_ref[:, first_row(k) : first_row(k) + n]
        lane = lax.broadcasted_iota(jnp.int32, (COLUMNS, n), 1)
        block = jnp.where(lane < 2 * degree + 1, block, jnp.zeros((), BF))
        for j0 in range(0, k + 1, GROUP):
            js = range(j0, min(k + 1, j0 + GROUP))
            halves = []
            for j in js:
                for p in range(2):
                    start = degree + SLOTS * j if p == 0 else degree - SLOTS * j - (SLOTS - 1)
                    base = FRONT + start * (k + 1)
                    if k == 0:
                        windows = [v_ref[pl.ds(base, SLOTS), :]]
                    else:
                        windows = [
                            v_ref[pl.ds(base + a, SLOTS, stride=k + 1), :] for a in range(k + 1)
                        ]
                    halves.append(jnp.concatenate([w.astype(BF) for w in windows], axis=1))
            y = lax.dot_general(
                jnp.concatenate(halves, axis=0),
                block,
                (((1,), (1,)), ((), ())),
                preferred_element_type=F32,
            )
            for j in js:
                for p in range(2):
                    row_at = (2 * (j - j0) + p) * SLOTS
                    part = y[row_at : row_at + SLOTS, :]
                    order = row if p == 0 else SLOTS - 1 - row
                    if j == k:
                        part = jnp.where(order <= slot_degree, part, 0.0)
                    if j == 0 and p == 1:
                        part = jnp.where(order >= 1, part, 0.0)
                    at = first_row(k) + (2 * j + p) * SLOTS
                    y_ref[at : at + SLOTS, :] = part

    def piece(k, j, p):
        at = first_row(k) + (2 * j + p) * SLOTS
        return y_ref[at : at + SLOTS, :].astype(BF)

    stores = []

    def send(lo, hi):
        lanes = pl.ds(lo, hi - lo)
        store = pltpu.make_async_copy(
            out_ref.at[:, lanes], out_hbm.at[:, lanes], sems.at[CLASSES + 1 + len(stores)]
        )
        store.start()
        stores.append(store)

    perms = [interleave(CLASSES), interleave(0)]
    for group in range(PAIRED):
        for p in range(2):
            stacked = jnp.concatenate([piece(k, j, p) for k, j in packed_rows(group)], axis=0)
            lanes = group * WIDE + p * COLUMNS
            out_ref[:, lanes : lanes + COLUMNS] = jnp.dot(
                perms[p], stacked, preferred_element_type=F32
            ).astype(BF)
        if group % 2:
            send((group - 1) * WIDE, (group + 1) * WIDE)
    stacked = jnp.concatenate(
        [piece(k, PAIRED, p) for p in range(2) for k in range(PAIRED, CLASSES)], axis=0
    )
    out_ref[:, PAIRED * WIDE :] = jnp.dot(
        interleave(PAIRED), stacked, preferred_element_type=F32
    ).astype(BF)
    send(PAIRED * WIDE, PACKED)
    for store in stores:
        store.wait()


def rotate(degree_slot, coefficients, rotations):
    scratch = [pltpu.VMEM((1, extent(k) * extent(k)), BF) for k in range(CLASSES)]
    top = extent(CLASSES - 1)
    scratch += [pltpu.VMEM((FRONT + top * CLASSES, 128), F32)] * 2
    scratch += [
        pltpu.VMEM((COLUMNS, first_row(CLASSES)), BF),
        pltpu.VMEM((first_row(CLASSES), COLUMNS), F32),
        pltpu.VMEM((CLASSES * SLOTS, PACKED), BF),
        pltpu.SemaphoreType.DMA((CLASSES + 4,)),
    ]
    return pl.pallas_call(
        rotate_kernel,
        out_shape=pltpu.HBM((CLASSES * SLOTS, PACKED), BF),
        in_specs=[
            pl.BlockSpec(memory_space=pltpu.SMEM),
            pl.BlockSpec(memory_space=pl.ANY),
            pl.BlockSpec(memory_space=pl.ANY),
        ],
        out_specs=pl.BlockSpec(memory_space=pltpu.HBM),
        scratch_shapes=scratch,
        compiler_params=pltpu.CompilerParams(vmem_limit_bytes=44 * MIB),
        cost_estimate=pl.CostEstimate(
            flops=4 * 10**9, bytes_accessed=18 * 10**6, transcendentals=0
        ),
        name="rotate",
    )(degree_slot, coefficients, rotations)


def scatter_kernel(grp_ref, legendre_ref, out_ref, rows_ref):
    lane = lax.broadcasted_iota(jnp.int32, (SLOTS, ORDERS), 1)

    def order_class(j):
        return legendre_ref[0, j * SLOTS : (j + 1) * SLOTS, :].astype(F32)

    def put(values, at):
        for i in range(values.shape[1] // 128):
            rows_ref[pl.ds(at + i, SLOTS, stride=BLOCKS), :] = values[:, i * 128 : (i + 1) * 128]

    for group in range(PAIRED):
        values = order_class(group)
        if group:
            other = pltpu.roll(order_class(CLASSES - group), SLOTS * group, 1)
            values = jnp.where(lane < SLOTS * group, other, values)
        put(values, group * ORDERS // 128)
    put(order_class(PAIRED)[:, SLOTS * PAIRED :], PAIRED * ORDERS // 128)
    out_ref[...] = rows_ref[...].astype(BF)


def scatter_rows(grp, legendre):
    return pl.pallas_call(
        scatter_kernel,
        grid_spec=pltpu.PrefetchScalarGridSpec(
            num_scalar_prefetch=1,
            grid=(1,),
            in_specs=[pl.BlockSpec((1, ORDERS, ORDERS), lambda i, grp: (grp[0], 0, 0))],
            out_specs=pl.BlockSpec((SLOTS * BLOCKS, 128), lambda i, grp: (0, 0)),
            scratch_shapes=[pltpu.VMEM((SLOTS * BLOCKS, 128), F32)],
        ),
        out_shape=jax.ShapeDtypeStruct((SLOTS * BLOCKS, 128), BF),
        compiler_params=pltpu.CompilerParams(vmem_limit_bytes=60 * MIB),
        name="scatter",
    )(grp, legendre)


def legendre_kernel(grp_ref, targets_ref, *refs):
    pieces = refs[:4]
    out_ref, wide_ref, rows_ref = refs[4:]
    for back in range(4):
        group = lax.rem(grp_ref[0] + 4 - back, 4)
        wide_ref[back] = pieces[back][...].astype(F32)
        for i in range(BLOCKS):
            rows_ref[
                pl.ds(pl.multiple_of(group * SLOTS, SLOTS), SLOTS), i * 128 : (i + 1) * 128
            ] = wide_ref[back, pl.ds(i, SLOTS, stride=BLOCKS), :].astype(BF)
    size = CLASSES * SLOTS

    def one_hot(which, depth):
        row = lax.broadcasted_iota(jnp.int32, (depth, size), 0)
        return jnp.where(row == targets_ref[which : which + 1, :], 1.0, 0.0).astype(BF)

    def put(at, left, right):
        out_ref[at * 4 * SLOTS : (at + 1) * 4 * SLOTS, :] = jnp.dot(
            left, right, preferred_element_type=F32
        ).astype(BF)

    main = one_hot(0, size)
    lane = lax.broadcasted_iota(jnp.int32, (4 * SLOTS, size), 1)
    for j in range(PAIRED):
        values = rows_ref[:, j * size : (j + 1) * size]
        kept = values
        if j:
            kept = jnp.where(lane >= SLOTS * j, values, jnp.zeros((), BF))
            put(CLASSES + 1 - j, values, one_hot(j, size))
        put(j, kept, main)
    values = rows_ref[:, PAIRED * size :]
    for p in range(2):
        put(PAIRED + p, values, one_hot(PAIRED + p, size // 2))


def legendre_rows(grp, targets, pieces):
    size = CLASSES * SLOTS
    return pl.pallas_call(
        legendre_kernel,
        out_shape=jax.ShapeDtypeStruct(((CLASSES + 1) * 4 * SLOTS, size), BF),
        in_specs=[pl.BlockSpec(memory_space=pltpu.SMEM)]
        + [pl.BlockSpec(memory_space=pltpu.VMEM)] * 5,
        out_specs=pl.BlockSpec(memory_space=pltpu.VMEM),
        scratch_shapes=[
            pltpu.VMEM((4, SLOTS * BLOCKS, 128), F32),
            pltpu.VMEM((4 * SLOTS, BLOCKS * 128), BF),
        ],
        compiler_params=pltpu.CompilerParams(vmem_limit_bytes=60 * MIB),
        cost_estimate=pl.CostEstimate(flops=10**9, bytes_accessed=4 * 10**6, transcendentals=0),
        name="legendre",
    )(grp, targets, *pieces)


def synthesize_kernel(x_ref, l_hbm, out_hbm, l_ref, f_ref, out_ref, sems):
    tall = 4 * SLOTS
    copies = []
    for i in range(CLASSES + 1):
        rows = pl.ds(i * tall, tall)
        copies.append(pltpu.make_async_copy(l_hbm.at[rows, :], l_ref.at[rows, :], sems.at[i]))
        copies[i].start()

    def put(j, left, lanes, width, at):
        summed = jnp.dot(
            l_ref[left * tall : (left + 1) * tall, :],
            x_ref[:, lanes : lanes + width],
            preferred_element_type=F32,
        )
        for g in range(4):
            for i in range(width // 128):
                f_ref[(g * WIDE + at) // 128 + i, pl.ds(j, SLOTS, stride=CLASSES), :] = summed[
                    g * SLOTS : (g + 1) * SLOTS, i * 128 : (i + 1) * 128
                ]

    for j in range(CLASSES):
        if j in (0, PAIRED):
            for i in range(j, PAIRED if j == 0 else CLASSES + 1):
                copies[i].wait()
        if j < PAIRED:
            put(j, j, j * WIDE, WIDE, 0)
        elif j == PAIRED:
            for p in range(2):
                put(j, PAIRED + p, PAIRED * WIDE, COLUMNS, p * COLUMNS)
        else:
            put(j, j + 1, (CLASSES - j) * WIDE, WIDE, 0)
    stores = []
    for g in range(OUTS):
        part = 4 * WIDE // OUTS
        for i in range(g * part // 128, (g + 1) * part // 128):
            out_ref[:, i * 128 : (i + 1) * 128] = f_ref[i].astype(BF)
        lanes = pl.ds(g * part, part)
        stores.append(
            pltpu.make_async_copy(
                out_ref.at[:, lanes], out_hbm.at[:, lanes], sems.at[CLASSES + 1 + g]
            )
        )
        stores[g].start()
    for store in stores:
        store.wait()


def synthesize(packed, rows):
    size = CLASSES * SLOTS
    return pl.pallas_call(
        synthesize_kernel,
        out_shape=pltpu.HBM((size, 4 * WIDE), BF),
        in_specs=[
            pl.BlockSpec(memory_space=pltpu.VMEM),
            pl.BlockSpec(memory_space=pltpu.HBM),
        ],
        out_specs=pl.BlockSpec(memory_space=pltpu.HBM),
        scratch_shapes=[
            pltpu.VMEM(rows.shape, BF),
            pltpu.VMEM((4 * WIDE // 128, size, 128), F32),
            pltpu.VMEM((size, 4 * WIDE), BF),
            pltpu.SemaphoreType.DMA((CLASSES + 5,)),
        ],
        compiler_params=pltpu.CompilerParams(vmem_limit_bytes=16 * MIB),
        cost_estimate=pl.CostEstimate(
            flops=2 * 10**9, bytes_accessed=7 * 10**6, transcendentals=0
        ),
        name="synthesize",
    )(
        packed,
        pltpu.with_memory_space_constraint(rows, pltpu.HBM),
    )


def transform_kernel(order_ref, x_ref, w_hbm, out_hbm, w_ref, lhs_ref, y_ref, out_ref, sems):
    width = NLON // STEPS
    waves = []
    for i in range(STEPS):
        lanes = pl.ds(i * width, width)
        waves.append(
            pltpu.make_async_copy(w_hbm.at[:, lanes], w_ref.at[:, lanes], sems.at[i])
        )
        waves[i].start()
    chosen = lax.broadcasted_iota(jnp.int32, (COLUMNS, COLUMNS), 1) == order_ref[...]
    chosen = jnp.where(chosen, 1.0, 0.0).astype(BF)
    for g in range(4):
        for p in range(2):
            lanes = g * WIDE + p * COLUMNS
            lhs_ref[g * COLUMNS : (g + 1) * COLUMNS, p * ORDERS : (p + 1) * ORDERS] = (
                lax.dot_general(
                    chosen,
                    x_ref[:, lanes : lanes + COLUMNS],
                    (((1,), (1,)), ((), ())),
                    preferred_element_type=F32,
                ).astype(BF)
            )
    stores = []
    for step in range(STEPS):
        waves[step].wait()
        total = jnp.dot(
            lhs_ref[...],
            w_ref[:, step * width : (step + 1) * width],
            preferred_element_type=F32,
        )
        for i in range(width // 128):
            at = step * width + i * 128
            for g in range(4):
                y_ref[step % 2, i, pl.ds(g, COLUMNS, stride=4), :] = total[
                    g * COLUMNS : (g + 1) * COLUMNS, i * 128 : (i + 1) * 128
                ]
            out_ref[:, :, at : at + 128] = (
                y_ref[step % 2, i].reshape(COLUMNS, 4, 128).astype(BF)
            )
        lanes = pl.ds(step * width, width)
        stores.append(
            pltpu.make_async_copy(
                out_ref.at[:, :, lanes], out_hbm.at[:, :, lanes], sems.at[STEPS + step]
            )
        )
        stores[step].start()
    for store in stores:
        store.wait()


def transform(column_order, received, wave):
    width = NLON // STEPS
    return pl.pallas_call(
        transform_kernel,
        out_shape=pltpu.HBM((COLUMNS, 4, NLON), BF),
        in_specs=[
            pl.BlockSpec(memory_space=pltpu.VMEM),
            pl.BlockSpec(memory_space=pltpu.VMEM),
            pl.BlockSpec(memory_space=pltpu.HBM),
        ],
        out_specs=pl.BlockSpec(memory_space=pltpu.HBM),
        scratch_shapes=[
            pltpu.VMEM(wave.shape, BF),
            pltpu.VMEM((4 * COLUMNS, 2 * ORDERS), BF),
            pltpu.VMEM((2, width // 128, 4 * COLUMNS, 128), F32),
            pltpu.VMEM((COLUMNS, 4, NLON), BF),
            pltpu.SemaphoreType.DMA((2 * STEPS,)),
        ],
        compiler_params=pltpu.CompilerParams(vmem_limit_bytes=20 * MIB),
        cost_estimate=pl.CostEstimate(
            flops=2 * 10**9, bytes_accessed=7 * 10**6, transcendentals=0
        ),
        name="transform",
    )(column_order, received, pltpu.with_memory_space_constraint(wave, pltpu.HBM))


def wave_table():
    row = jnp.arange(ORDERS, dtype=jnp.int32)
    order = SLOTS * (row % CLASSES) + row // CLASSES
    longitude = jnp.arange(NLON, dtype=jnp.int32)
    angles = (order[:, None] * longitude[None, :] % NLON).astype(F32) * (2.0 * math.pi / NLON)
    return (jnp.concatenate([jnp.cos(angles), jnp.sin(angles)], axis=0) / ORDERS).astype(BF)


def one_hot_targets(degree_slot):
    slot_major = degree_slot.T
    row = jnp.arange(CLASSES, dtype=jnp.int32)[None, :]
    main = slot_major + SLOTS * row
    targets = [main]
    for group in range(1, PAIRED):
        shifted = jnp.roll(slot_major, group - CLASSES, axis=1) + SLOTS * row
        targets.append(jnp.where(row < group, shifted, -1))
    half = jnp.roll(slot_major, -PAIRED, axis=1) + SLOTS * row
    targets.append(jnp.where(row < PAIRED, half, -1))
    half = slot_major + SLOTS * (row - PAIRED)
    targets.append(jnp.where(row >= PAIRED, half, -1))
    targets += [main, main]
    return jnp.stack(targets, axis=0).reshape(CLASSES, CLASSES * SLOTS)


def local(coefficients, rotations, legendre, degree_slot, column_order):
    grp = lax.axis_index("grp")
    sent = scatter_rows(grp.reshape(1), legendre).reshape(SLOTS, BLOCKS // 2, 2, 128)
    mine = lax.all_to_all(sent, "own", split_axis=0, concat_axis=0, tiled=True)
    pieces = [mine]
    for shift in range(1, 4):
        pieces.append(lax.ppermute(mine, "grp", [(i, (i + shift) % 4) for i in range(4)]))
    pieces = [piece.reshape(SLOTS * BLOCKS, 128) for piece in pieces]
    rows = legendre_rows(grp.reshape(1), one_hot_targets(degree_slot), pieces)

    outgoing = rotate(
        degree_slot, coefficients.reshape(COLUMNS, -1), rotations
    )
    packed = lax.all_to_all(
        outgoing.reshape(SLOTS, CLASSES, PACKED), "own", split_axis=0, concat_axis=0, tiled=True
    )
    fourier = synthesize(packed.reshape(SLOTS * CLASSES, PACKED), rows)
    received = lax.all_to_all(
        fourier.reshape(SLOTS, CLASSES, 4 * WIDE), "own", split_axis=0, concat_axis=0, tiled=True
    )
    return transform(
        column_order.reshape(-1, 1), received.reshape(SLOTS * CLASSES, 4 * WIDE), wave_table()
    )


def solution(mesh):
    placed = (P("own", "grp", None), P("own", None), P("own", None, None), P(), P("grp"))
    return jax.shard_map(
        local, mesh=mesh, in_specs=placed, out_specs=P("grp", "own", None), check_vma=False
    )
```

```python
import functools
import math

import jax
import jax.numpy as jnp
from jax import lax
from jax.experimental import pallas as pl
from jax.experimental.pallas import tpu as pltpu
from jax.sharding import PartitionSpec as P

SLOTS = 64
CLASSES = 8
COLUMNS = 256
ORDERS = SLOTS * CLASSES
NLON = 2 * ORDERS
PAIRED = CLASSES // 2
WIDE = 2 * COLUMNS
STEPS = 2
GROUP = 2
OUTS = 4
WAITS = {0: (0, 1), 2: (2, 3, 4)}
PACKED = PAIRED * WIDE + COLUMNS
FRONT = SLOTS * CLASSES
BLOCKS = (PAIRED * ORDERS + ORDERS // 2) // 128
BF = jnp.bfloat16
F32 = jnp.float32
MIB = 1024 * 1024


def extent(k):
    return 2 * SLOTS * (k + 1)


def first_row(k):
    return SLOTS * k * (k + 1)


def rotation_offset(k):
    return 4 * SLOTS * SLOTS * k * (k + 1) * (2 * k + 1) // 6


def packed_rows(group):
    if group == 0:
        return [(r, 0) for r in range(CLASSES)]
    other = CLASSES - group
    return [(r, group) if r >= group else (r + other, other) for r in range(CLASSES)]


def interleave(reverse_from):
    size = CLASSES * SLOTS
    row = lax.broadcasted_iota(jnp.int32, (size, size), 0)
    col = lax.broadcasted_iota(jnp.int32, (size, size), 1)
    d = row // CLASSES
    r = row % CLASSES
    d = jnp.where(r >= reverse_from, SLOTS - 1 - d, d)
    return jnp.where(col == r * SLOTS + d, 1.0, 0.0).astype(BF)


def rotate_kernel(deg_ref, coef_hbm, rot_ref, out_hbm, *scratch):
    flats = scratch[:CLASSES]
    wide = scratch[CLASSES : CLASSES + 2]
    coef_ref, y_ref, out_ref, sems = scratch[CLASSES + 2 :]
    own = lax.axis_index("own")
    copies = []
    first = pltpu.make_async_copy(coef_hbm, coef_ref, sems.at[CLASSES])
    for k in range(CLASSES):
        size = extent(k) * extent(k)
        copies.append(
            pltpu.make_async_copy(
                rot_ref.at[:, pl.ds(rotation_offset(k), size)], flats[k], sems.at[k]
            )
        )
    for at, k in enumerate(range(CLASSES)):
        copies[k].start()
        if at == 1:
            first.start()
    row = lax.broadcasted_iota(jnp.int32, (SLOTS, COLUMNS), 0)
    lane = lax.broadcasted_iota(jnp.int32, (COLUMNS, 128), 1)
    for at, k in enumerate(range(CLASSES)):
        n = extent(k)
        rows = n * (k + 1)
        v_ref = wide[at % 2]
        copies[k].wait()
        v_ref[FRONT : FRONT + rows, :] = flats[k][...].reshape(rows, 128).astype(F32)
        slot_degree = deg_ref[k, own]
        degree = SLOTS * k + slot_degree
        if k == 0:
            first.wait()
        tail = pl.ds(first_row(k) + n - 128, 128)
        coef_ref[:, tail] = jnp.where(
            lane < 2 * slot_degree + 1, coef_ref[:, tail], jnp.zeros((), BF)
        )
        for j0 in range(0, k + 1, GROUP):
            js = range(j0, min(k + 1, j0 + GROUP))
            halves = []
            for j in js:
                for p in range(2):
                    start = degree + SLOTS * j if p == 0 else degree - SLOTS * j - (SLOTS - 1)
                    base = FRONT + start * (k + 1)
                    if k == 0:
                        windows = [v_ref[pl.ds(base, SLOTS), :]]
                    else:
                        windows = [
                            v_ref[pl.ds(base + a, SLOTS, stride=k + 1), :] for a in range(k + 1)
                        ]
                    halves.append(jnp.concatenate([w.astype(BF) for w in windows], axis=1))
            y = lax.dot_general(
                jnp.concatenate(halves, axis=0),
                coef_ref[:, first_row(k) : first_row(k) + n],
                (((1,), (1,)), ((), ())),
                preferred_element_type=F32,
            )
            for j in js:
                for p in range(2):
                    row_at = (2 * (j - j0) + p) * SLOTS
                    part = y[row_at : row_at + SLOTS, :]
                    order = row if p == 0 else SLOTS - 1 - row
                    if j == k:
                        part = jnp.where(order <= slot_degree, part, 0.0)
                    if j == 0 and p == 1:
                        part = jnp.where(order >= 1, part, 0.0)
                    at = first_row(k) + (2 * j + p) * SLOTS
                    y_ref[at : at + SLOTS, :] = part

    def piece(k, j, p):
        at = first_row(k) + (2 * j + p) * SLOTS
        return y_ref[at : at + SLOTS, :].astype(BF)

    stores = []

    def send(lo, hi):
        lanes = pl.ds(lo, hi - lo)
        store = pltpu.make_async_copy(
            out_ref.at[:, lanes], out_hbm.at[:, lanes], sems.at[CLASSES + 1 + len(stores)]
        )
        store.start()
        stores.append(store)

    perms = [interleave(CLASSES), interleave(0)]
    for group in range(PAIRED):
        for p in range(2):
            stacked = jnp.concatenate([piece(k, j, p) for k, j in packed_rows(group)], axis=0)
            lanes = group * WIDE + p * COLUMNS
            out_ref[:, lanes : lanes + COLUMNS] = jnp.dot(
                perms[p], stacked, preferred_element_type=F32
            ).astype(BF)
        if group % 2:
            send((group - 1) * WIDE, (group + 1) * WIDE)
    stacked = jnp.concatenate(
        [piece(k, PAIRED, p) for p in range(2) for k in range(PAIRED, CLASSES)], axis=0
    )
    out_ref[:, PAIRED * WIDE :] = jnp.dot(
        interleave(PAIRED), stacked, preferred_element_type=F32
    ).astype(BF)
    send(PAIRED * WIDE, PACKED)
    for store in stores:
        store.wait()


def rotate(degree_slot, coefficients, rotations):
    scratch = [pltpu.VMEM((1, extent(k) * extent(k)), BF) for k in range(CLASSES)]
    top = extent(CLASSES - 1)
    scratch += [pltpu.VMEM((FRONT + top * CLASSES, 128), F32)] * 2
    scratch += [
        pltpu.VMEM((COLUMNS, first_row(CLASSES)), BF),
        pltpu.VMEM((first_row(CLASSES), COLUMNS), F32),
        pltpu.VMEM((CLASSES * SLOTS, PACKED), BF),
        pltpu.SemaphoreType.DMA((CLASSES + 4,)),
    ]
    return pl.pallas_call(
        rotate_kernel,
        out_shape=pltpu.HBM((CLASSES * SLOTS, PACKED), BF),
        in_specs=[
            pl.BlockSpec(memory_space=pltpu.SMEM),
            pl.BlockSpec(memory_space=pl.ANY),
            pl.BlockSpec(memory_space=pl.ANY),
        ],
        out_specs=pl.BlockSpec(memory_space=pltpu.HBM),
        scratch_shapes=scratch,
        compiler_params=pltpu.CompilerParams(vmem_limit_bytes=44 * MIB),
        cost_estimate=pl.CostEstimate(
            flops=4 * 10**9, bytes_accessed=18 * 10**6, transcendentals=0
        ),
        name="rotate",
    )(degree_slot, coefficients, rotations)


def scatter_kernel(grp_ref, legendre_ref, out_ref, rows_ref):
    lane = lax.broadcasted_iota(jnp.int32, (SLOTS, ORDERS), 1)

    def order_class(j):
        return legendre_ref[0, j * SLOTS : (j + 1) * SLOTS, :].astype(F32)

    def put(values, at):
        for i in range(values.shape[1] // 128):
            rows_ref[pl.ds(at + i, SLOTS, stride=BLOCKS), :] = values[:, i * 128 : (i + 1) * 128]

    for group in range(PAIRED):
        values = order_class(group)
        if group:
            other = pltpu.roll(order_class(CLASSES - group), SLOTS * group, 1)
            values = jnp.where(lane < SLOTS * group, other, values)
        put(values, group * ORDERS // 128)
    put(order_class(PAIRED)[:, SLOTS * PAIRED :], PAIRED * ORDERS // 128)
    out_ref[...] = rows_ref[...].astype(BF)


def scatter_rows(grp, legendre):
    return pl.pallas_call(
        scatter_kernel,
        grid_spec=pltpu.PrefetchScalarGridSpec(
            num_scalar_prefetch=1,
            grid=(1,),
            in_specs=[pl.BlockSpec((1, ORDERS, ORDERS), lambda i, grp: (grp[0], 0, 0))],
            out_specs=pl.BlockSpec((SLOTS * BLOCKS, 128), lambda i, grp: (0, 0)),
            scratch_shapes=[pltpu.VMEM((SLOTS * BLOCKS, 128), F32)],
        ),
        out_shape=jax.ShapeDtypeStruct((SLOTS * BLOCKS, 128), BF),
        compiler_params=pltpu.CompilerParams(vmem_limit_bytes=60 * MIB),
        name="scatter",
    )(grp, legendre)


def legendre_kernel(grp_ref, targets_ref, *refs):
    pieces = refs[:4]
    out_ref, wide_ref, rows_ref = refs[4:]
    for back in range(4):
        group = lax.rem(grp_ref[0] + 4 - back, 4)
        wide_ref[back] = pieces[back][...].astype(F32)
        for i in range(BLOCKS):
            rows_ref[
                pl.ds(pl.multiple_of(group * SLOTS, SLOTS), SLOTS), i * 128 : (i + 1) * 128
            ] = wide_ref[back, pl.ds(i, SLOTS, stride=BLOCKS), :].astype(BF)
    size = CLASSES * SLOTS

    def one_hot(which, depth):
        row = lax.broadcasted_iota(jnp.int32, (depth, size), 0)
        return jnp.where(row == targets_ref[which : which + 1, :], 1.0, 0.0).astype(BF)

    def picked(left, right):
        return jnp.dot(left, right, preferred_element_type=F32)

    main = one_hot(0, size)
    lane = lax.broadcasted_iota(jnp.int32, (4 * SLOTS, size), 1)
    for group in range(PAIRED + 1):
        values = rows_ref[:, group * size : group * size + (size if group < PAIRED else size // 2)]
        if group == 0:
            merged = picked(values, main)
        elif group < PAIRED:
            kept = jnp.where(lane >= SLOTS * group, values, jnp.zeros((), BF))
            merged = picked(kept, main) + picked(values, one_hot(group, size))
        else:
            merged = picked(values, one_hot(PAIRED, size // 2)) + picked(
                values, one_hot(PAIRED + 1, size // 2)
            )
        out_ref[group * 4 * SLOTS : (group + 1) * 4 * SLOTS, :] = merged.astype(BF)


def legendre_rows(grp, targets, pieces):
    size = CLASSES * SLOTS
    return pl.pallas_call(
        legendre_kernel,
        out_shape=jax.ShapeDtypeStruct(((PAIRED + 1) * 4 * SLOTS, size), BF),
        in_specs=[pl.BlockSpec(memory_space=pltpu.SMEM)]
        + [pl.BlockSpec(memory_space=pltpu.VMEM)] * 5,
        out_specs=pl.BlockSpec(memory_space=pltpu.VMEM),
        scratch_shapes=[
            pltpu.VMEM((4, SLOTS * BLOCKS, 128), F32),
            pltpu.VMEM((4 * SLOTS, BLOCKS * 128), BF),
        ],
        compiler_params=pltpu.CompilerParams(vmem_limit_bytes=60 * MIB),
        cost_estimate=pl.CostEstimate(flops=10**9, bytes_accessed=4 * 10**6, transcendentals=0),
        name="legendre",
    )(grp, targets, *pieces)


def synthesize_kernel(x_ref, l_hbm, out_hbm, l_ref, f_ref, out_ref, sems):
    tall = 4 * SLOTS
    copies = []
    for i in range(PAIRED + 1):
        rows = pl.ds(i * tall, tall)
        copies.append(pltpu.make_async_copy(l_hbm.at[rows, :], l_ref.at[rows, :], sems.at[i]))
        copies[i].start()
    r = lax.broadcasted_iota(jnp.int32, (tall, CLASSES * SLOTS), 1) % CLASSES

    def put(j, group, keep, width, at):
        left = l_ref[group * tall : (group + 1) * tall, :]
        if keep is not None:
            left = jnp.where(keep, left, jnp.zeros((), BF))
        summed = jnp.dot(
            left, x_ref[:, group * WIDE : group * WIDE + width], preferred_element_type=F32
        )
        for g in range(4):
            for i in range(width // 128):
                f_ref[(g * WIDE + at) // 128 + i, pl.ds(j, SLOTS, stride=CLASSES), :] = summed[
                    g * SLOTS : (g + 1) * SLOTS, i * 128 : (i + 1) * 128
                ]

    for group in range(PAIRED + 1):
        for i in WAITS.get(group, ()):
            copies[i].wait()
        if group == 0:
            put(0, 0, None, WIDE, 0)
        elif group < PAIRED:
            put(group, group, r >= group, WIDE, 0)
            put(CLASSES - group, group, r < group, WIDE, 0)
        else:
            put(PAIRED, group, r < PAIRED, COLUMNS, 0)
            put(PAIRED, group, r >= PAIRED, COLUMNS, COLUMNS)
    stores = []
    for g in range(OUTS):
        part = 4 * WIDE // OUTS
        for i in range(g * part // 128, (g + 1) * part // 128):
            out_ref[:, i * 128 : (i + 1) * 128] = f_ref[i].astype(BF)
        lanes = pl.ds(g * part, part)
        stores.append(
            pltpu.make_async_copy(
                out_ref.at[:, lanes], out_hbm.at[:, lanes], sems.at[PAIRED + 1 + g]
            )
        )
        stores[g].start()
    for store in stores:
        store.wait()


def synthesize(packed, rows):
    size = CLASSES * SLOTS
    return pl.pallas_call(
        synthesize_kernel,
        out_shape=pltpu.HBM((size, 4 * WIDE), BF),
        in_specs=[
            pl.BlockSpec(memory_space=pltpu.VMEM),
            pl.BlockSpec(memory_space=pltpu.HBM),
        ],
        out_specs=pl.BlockSpec(memory_space=pltpu.HBM),
        scratch_shapes=[
            pltpu.VMEM(rows.shape, BF),
            pltpu.VMEM((4 * WIDE // 128, size, 128), F32),
            pltpu.VMEM((size, 4 * WIDE), BF),
            pltpu.SemaphoreType.DMA((PAIRED + 5,)),
        ],
        compiler_params=pltpu.CompilerParams(vmem_limit_bytes=16 * MIB),
        cost_estimate=pl.CostEstimate(
            flops=2 * 10**9, bytes_accessed=7 * 10**6, transcendentals=0
        ),
        name="synthesize",
    )(
        packed,
        pltpu.with_memory_space_constraint(rows, pltpu.HBM),
    )


def transform_kernel(order_ref, x_ref, w_hbm, out_hbm, w_ref, lhs_ref, y_ref, out_ref, sems):
    width = NLON // STEPS
    waves = []
    for i in range(STEPS):
        lanes = pl.ds(i * width, width)
        waves.append(
            pltpu.make_async_copy(w_hbm.at[:, lanes], w_ref.at[:, lanes], sems.at[i])
        )
        waves[i].start()
    chosen = lax.broadcasted_iota(jnp.int32, (COLUMNS, COLUMNS), 1) == order_ref[...]
    chosen = jnp.where(chosen, 1.0, 0.0).astype(BF)
    for g in range(4):
        for p in range(2):
            lanes = g * WIDE + p * COLUMNS
            lhs_ref[g * COLUMNS : (g + 1) * COLUMNS, p * ORDERS : (p + 1) * ORDERS] = (
                lax.dot_general(
                    chosen,
                    x_ref[:, lanes : lanes + COLUMNS],
                    (((1,), (1,)), ((), ())),
                    preferred_element_type=F32,
                ).astype(BF)
            )
    stores = []
    for step in range(STEPS):
        waves[step].wait()
        total = jnp.dot(
            lhs_ref[...],
            w_ref[:, step * width : (step + 1) * width],
            preferred_element_type=F32,
        )
        for i in range(width // 128):
            at = step * width + i * 128
            for g in range(4):
                y_ref[step % 2, i, pl.ds(g, COLUMNS, stride=4), :] = total[
                    g * COLUMNS : (g + 1) * COLUMNS, i * 128 : (i + 1) * 128
                ]
            out_ref[:, :, at : at + 128] = (
                y_ref[step % 2, i].reshape(COLUMNS, 4, 128).astype(BF)
            )
        lanes = pl.ds(step * width, width)
        stores.append(
            pltpu.make_async_copy(
                out_ref.at[:, :, lanes], out_hbm.at[:, :, lanes], sems.at[STEPS + step]
            )
        )
        stores[step].start()
    for store in stores:
        store.wait()


def transform(column_order, received, wave):
    width = NLON // STEPS
    return pl.pallas_call(
        transform_kernel,
        out_shape=pltpu.HBM((COLUMNS, 4, NLON), BF),
        in_specs=[
            pl.BlockSpec(memory_space=pltpu.VMEM),
            pl.BlockSpec(memory_space=pltpu.VMEM),
            pl.BlockSpec(memory_space=pltpu.HBM),
        ],
        out_specs=pl.BlockSpec(memory_space=pltpu.HBM),
        scratch_shapes=[
            pltpu.VMEM(wave.shape, BF),
            pltpu.VMEM((4 * COLUMNS, 2 * ORDERS), BF),
            pltpu.VMEM((2, width // 128, 4 * COLUMNS, 128), F32),
            pltpu.VMEM((COLUMNS, 4, NLON), BF),
            pltpu.SemaphoreType.DMA((2 * STEPS,)),
        ],
        compiler_params=pltpu.CompilerParams(vmem_limit_bytes=20 * MIB),
        cost_estimate=pl.CostEstimate(
            flops=2 * 10**9, bytes_accessed=7 * 10**6, transcendentals=0
        ),
        name="transform",
    )(column_order, received, pltpu.with_memory_space_constraint(wave, pltpu.HBM))


def wave_table():
    row = jnp.arange(ORDERS, dtype=jnp.int32)
    order = SLOTS * (row % CLASSES) + row // CLASSES
    longitude = jnp.arange(NLON, dtype=jnp.int32)
    angles = (order[:, None] * longitude[None, :] % NLON).astype(F32) * (2.0 * math.pi / NLON)
    return (jnp.concatenate([jnp.cos(angles), jnp.sin(angles)], axis=0) / ORDERS).astype(BF)


def one_hot_targets(degree_slot):
    slot_major = degree_slot.T
    row = jnp.arange(CLASSES, dtype=jnp.int32)[None, :]
    main = slot_major + SLOTS * row
    targets = [main]
    for group in range(1, PAIRED):
        shifted = jnp.roll(slot_major, group - CLASSES, axis=1) + SLOTS * row
        targets.append(jnp.where(row < group, shifted, -1))
    half = jnp.roll(slot_major, -PAIRED, axis=1) + SLOTS * row
    targets.append(jnp.where(row < PAIRED, half, -1))
    half = slot_major + SLOTS * (row - PAIRED)
    targets.append(jnp.where(row >= PAIRED, half, -1))
    targets += [main, main]
    return jnp.stack(targets, axis=0).reshape(CLASSES, CLASSES * SLOTS)


def local(coefficients, rotations, legendre, degree_slot, column_order):
    grp = lax.axis_index("grp")
    sent = scatter_rows(grp.reshape(1), legendre).reshape(SLOTS, BLOCKS // 2, 2, 128)
    mine = lax.all_to_all(sent, "own", split_axis=0, concat_axis=0, tiled=True)
    pieces = [mine]
    for shift in range(1, 4):
        pieces.append(lax.ppermute(mine, "grp", [(i, (i + shift) % 4) for i in range(4)]))
    pieces = [piece.reshape(SLOTS * BLOCKS, 128) for piece in pieces]
    rows = legendre_rows(grp.reshape(1), one_hot_targets(degree_slot), pieces)

    outgoing = rotate(
        degree_slot, coefficients.reshape(COLUMNS, -1), rotations
    )
    packed = lax.all_to_all(
        outgoing.reshape(SLOTS, CLASSES, PACKED), "own", split_axis=0, concat_axis=0, tiled=True
    )
    fourier = synthesize(packed.reshape(SLOTS * CLASSES, PACKED), rows)
    received = lax.all_to_all(
        fourier.reshape(SLOTS, CLASSES, 4 * WIDE), "own", split_axis=0, concat_axis=0, tiled=True
    )
    return transform(
        column_order.reshape(-1, 1), received.reshape(SLOTS * CLASSES, 4 * WIDE), wave_table()
    )


def solution(mesh):
    placed = (P("own", "grp", None), P("own", None), P("own", None, None), P(), P("grp"))
    return jax.shard_map(
        local, mesh=mesh, in_specs=placed, out_specs=P("grp", "own", None), check_vma=False
    )
```
